32 devices in a mesh: win: 2 (over y), tm: 4 (over z), pix: 4 (over x, core).
Axes of the slice: x: 2, y: 2, z: 4, core: 2. Of those that a mesh axis runs over, the one named last changes fastest.
Arguments:
- intensity: bfloat16 [1024, 12288], P(('win', 'tm'), 'pix'), parts along dimension 0, may hold values from 0.049804688 to 4
- cycle_labels: int32 [12288], P('pix'), may hold values from 0 to 1, as said below
Outputs:
- two_time: float32 [4, 512, 512], P('win', 'tm', 'pix'), parts along dimension 0
The draws below stay inside these ranges and needn't reach their ends.
There are 2 independent parts, one for each index of `win`. The reference program is written for one: setup_inputs(seed, part) draws one part's arguments, and reference() takes and returns one part's arrays. A program takes and returns all parts, laid end to end along the dimension named above; an argument that names none is the same for every part. Nothing has to cross between parts.
Inputs may be any that keep to these rules, and one draw needn't show every extreme that they name: `cycle_labels`: each aligned block of 3072 pixels holds exactly 1536 pixels of every cycle.
All inputs are finite; a program needn't handle non-finite values.
Results may differ from the reference program's by a relative error of at most 0.0003.
Values may be sent and summed in bfloat16 or wider, within the bound.
No kernel may reach another device: no remote copies, remote signals or barrier semaphores. Data moves between devices by JAX's collectives and lax.ppermute only.
A program may use at most 64 MiB of HBM per device.

```python
import jax
import jax.numpy as jnp
from jax import lax

CYCLES = 2
CYCLE_PIX = 6144
FRAMES = 512
PIXELS = 12288
PIX_DEV = 3072


def draw_cycle_labels(key, part):
    blocks = PIXELS // PIX_DEV
    keys = jax.random.split(key, blocks)
    perms = jax.vmap(lambda k: jax.random.permutation(k, PIX_DEV))(keys)
    return (perms % CYCLES).astype(jnp.int32).reshape(PIXELS)


def level_of(rng, dims, cuts, low, top_value):
    def one(position, parts):
        heights = jax.random.uniform(jax.random.fold_in(jax.random.fold_in(rng, 6), position), (parts,), jnp.float32, low / len(cuts), top_value / len(cuts))
        return jnp.repeat(jnp.exp(heights), dims[position] // parts).reshape((-1,) + (1,) * (len(dims) - position - 1))

    factor_of = one(*cuts[0])
    for cut in cuts[1:]:
        factor_of = factor_of * one(*cut)
    return factor_of


def setup_inputs(seed: int = 0, part: int = 0) -> dict:
    arg_keys = jax.random.split(jax.random.key(seed), 3)
    part_splits = jax.random.split(jax.random.fold_in(arg_keys[2], part), 3)
    return {
        "intensity": jnp.clip(0.049804688 + 3.9501953 * jax.random.uniform(part_splits[0], (FRAMES, PIXELS), jnp.float32) ** level_of(part_splits[0], (FRAMES, PIXELS), ((0, 4), (1, 4)), -0.2, 0.2), 0.049804688, 4.0).astype(jnp.bfloat16),
        "cycle_labels": draw_cycle_labels(jax.random.fold_in(arg_keys[2], 71), part),
    }


def reference(intensity, cycle_labels):
    order = jnp.argsort(cycle_labels, stable=True)
    grouped = jnp.take(intensity, order, axis=1).astype(jnp.float32)
    grouped = jnp.transpose(grouped.reshape(FRAMES, CYCLES, CYCLE_PIX), (1, 0, 2))
    sums = jnp.sum(grouped, axis=2)

    def one_cycle(index):
        block = grouped[index]
        return jnp.dot(block, block.T, precision=lax.Precision.HIGHEST, preferred_element_type=jnp.float32)

    gram = lax.map(one_cycle, jnp.arange(CYCLES, dtype=jnp.int32))
    return CYCLE_PIX * gram / (sums[:, :, None] * sums[:, None, :])
```

```python
import functools

import jax
import jax.numpy as jnp
import numpy as np
from jax import lax
from jax.experimental import pallas as pl
from jax.experimental.pallas import tpu as pltpu
from jax.sharding import PartitionSpec as P

CYCLES = 2
SUM_ROWS = 16
TILE, ENDS, EARLY = 0, 1, 2
CONTRACT_LAST = (((1,), (1,)), ((), ()))


def masks_of(labels, rows):
    cycle = lax.broadcasted_iota(jnp.int32, (rows, labels.shape[-1]), 0)
    return (cycle == labels).astype(jnp.float32).astype(jnp.bfloat16)


def masked(block, masks):
    return [block * masks[q : q + 1, :] for q in range(CYCLES)]


def products(left, right):
    return lax.dot_general(left, right, CONTRACT_LAST, preferred_element_type=jnp.float32)


def own_kernel(x_ref, labels_ref, out_ref):
    x = x_ref[...]
    masks = masks_of(labels_ref[...], SUM_ROWS)
    left = jnp.concatenate(masked(x, masks) + [masks], axis=0)
    out_ref[...] = products(left, x)


def near_kernel(pick_ref, x_ref, labels_ref, first_ref, second_ref, own_ref, send_ref, keep_ref):
    x = x_ref[...]
    half = first_ref.shape[1]
    rows = CYCLES * x.shape[0]
    left = jnp.concatenate(masked(x, masks_of(labels_ref[...], SUM_ROWS)), axis=0)
    near = products(left[:, :half], first_ref[...]) + products(left[:, half:], second_ref[...])
    own = own_ref[:rows, :]
    stays = pick_ref[0] == 1
    send_ref[:rows, :] = jnp.where(stays, near, own)
    keep_ref[:rows, :] = jnp.where(stays, own, near)
    send_ref[rows:, :] = own_ref[rows:, :]
    keep_ref[rows:, :] = own_ref[rows:, :]


def far_first_kernel(x_ref, ends_ref, labels_ref, far_ref, out_ref):
    masks = masks_of(labels_ref[...], SUM_ROWS)
    left = jnp.concatenate(masked(x_ref[...], masks) + masked(ends_ref[...], masks), axis=0)
    out_ref[...] = products(left, far_ref[...])


def far_second_kernel(pick_ref, x_ref, ends_ref, labels_ref, far_ref, sofar_ref, early_ref, *rest):
    outs, keep_ref, tiles = rest[:-2], rest[-2], rest[-1]
    masks = masks_of(labels_ref[...], SUM_ROWS)
    rows = early_ref.shape[0]
    left = jnp.concatenate(masked(x_ref[...], masks) + masked(ends_ref[...], masks), axis=0)
    far = sofar_ref[...] + products(left, far_ref[...])
    tiles[TILE] = far[:rows, :]
    tiles[ENDS] = far[rows:, :]
    tiles[EARLY] = early_ref[...]
    keep_ref[...] = jnp.where(pick_ref[0] == 1, far[:rows, :], 0.0)
    for slot, out_ref in enumerate(outs):
        out_ref[...] = tiles[pick_ref[1 + slot]]


def final_kernel(pix_total, pick_ref, early_ref, keep_ref, a_ref, b_ref, c_ref, d_ref, sums_ref, swapped_ref, out_ref):
    frames = out_ref.shape[1]
    sums = sums_ref[...]
    columns = jnp.where(pick_ref[0] == 1, sums, swapped_ref[...])
    for q in range(CYCLES):
        part = slice(q * frames, (q + 1) * frames)
        turned = a_ref[part, :] + b_ref[part, :]
        gram = early_ref[part, :] + keep_ref[part, :] + c_ref[part, :] + d_ref[part, :] + turned.T
        row_sum = jnp.broadcast_to(sums[q : q + 1, :], (frames, frames)).T
        out_ref[q] = (pix_total // CYCLES) * gram / (row_sum * columns[q : q + 1, :])


def vmem_call(kernel, out_shapes, in_specs, name, flops, bytes_accessed, scratch=()):
    many = isinstance(out_shapes, (list, tuple))
    whole = pl.BlockSpec(memory_space=pltpu.VMEM)
    return pl.pallas_call(
        kernel,
        out_shape=out_shapes,
        grid=(1,),
        in_specs=in_specs,
        out_specs=[whole] * len(out_shapes) if many else whole,
        scratch_shapes=scratch,
        name=name,
        compiler_params=pltpu.CompilerParams(vmem_limit_bytes=24 * 2**20),
        cost_estimate=pl.CostEstimate(flops=flops, bytes_accessed=bytes_accessed, transcendentals=0),
    )


class Plan:
    def __init__(self, blocks):
        self.blocks = blocks
        self.last = blocks - 1
        self.devices = [(z, x, c) for z in range(blocks) for x in range(2) for c in range(2)]

    def index(self, place):
        z, x, c = place
        return z * 4 + x * 2 + c

    def pairs(self, rule):
        found = []
        for place in self.devices:
            target = rule(*place)
            if target is not None:
                found.append((self.index(place), self.index(target)))
        return found

    def shift(self, z, x, c):
        t = z + 1 - 2 * c
        return (t, x, c) if 0 <= t <= self.last else None

    def relay(self, z, x, c):
        t = z + 1 - 2 * c
        return (t, x, c) if 0 <= t <= self.last and z in (1, 2) else None

    def ends(self, z, x, c):
        if (z, c) == (self.last, 0):
            return (z - 1, x, c)
        if (z, c) == (0, 1):
            return (1, x, c)
        return None

    def core(self, z, x, c):
        return (z, x, 1 - c)

    def side(self, z, x, c):
        return (z, 1 - x, c)

    def swap(self, z, x, c):
        pix = 2 * x + c
        return None if pix == z else (pix, z // 2, z % 2)

    def late(self):
        a, b, c, d = (2, 0, 0), (2, 1, 0), (0, 0, 1), (0, 1, 1)
        lower, upper = (0, 1, 0), (2, 0, 0)
        corner, other = (0, 1, 1), (3, 0, 0)
        slots = [
            {b: (lower, TILE), c: (upper, TILE), a: (corner, ENDS)},
            {a: (lower, TILE), d: (upper, TILE), b: (corner, ENDS)},
            {b: (upper, TILE), c: (lower, TILE), a: (other, ENDS)},
            {d: (lower, TILE), b: (other, ENDS)},
        ]

        def mirror(place):
            z, x, k = place
            return (self.last - z, 1 - x, 1 - k)

        full = []
        for slot in slots:
            both = dict(slot)
            for source, (target, tile) in slot.items():
                both[mirror(source)] = (mirror(target), tile)
            full.append(both)
        for place in self.devices:
            target = self.swap(*place)
            if target is not None and abs(target[0] - place[0]) == 1:
                full[1][place] = (target, EARLY)
        return full

    def table(self):
        late = self.late()
        rows = []
        for place in self.devices:
            z, x, c = place
            stays = int(z % 2 == c)
            near_side = int(x == z // 2)
            diagonal = int(2 * x + c == z)
            keep = int(place in ((2, 0, 0), (1, 1, 1)))
            picks = [slot[place][1] if place in slot else TILE for slot in late]
            rows.append([stays, near_side, diagonal, 0, keep] + picks)
        return np.asarray(rows, np.int32)


def planned_body(intensity, cycle_labels):
    frames, pix_dev = intensity.shape
    half = pix_dev // 2
    pix_total = pix_dev * lax.axis_size("pix")
    plan = Plan(lax.axis_size("tm"))
    line = ("tm", "pix")

    def send(value, rule):
        return lax.ppermute(value, line, plan.pairs(rule))

    picks = jnp.asarray(plan.table())[lax.axis_index(line)]
    labels = cycle_labels.reshape(1, pix_dev)
    whole = pl.BlockSpec(memory_space=pltpu.VMEM)
    scalars = pl.BlockSpec(memory_space=pltpu.SMEM)
    left = pl.BlockSpec((frames, half), lambda step: (0, 0))
    right = pl.BlockSpec((frames, half), lambda step: (0, 1))
    left_labels = pl.BlockSpec((1, half), lambda step: (0, 0))
    right_labels = pl.BlockSpec((1, half), lambda step: (0, 1))
    rows = CYCLES * frames
    tile = jax.ShapeDtypeStruct((rows, frames), jnp.float32)
    tile_sums = jax.ShapeDtypeStruct((rows + SUM_ROWS, frames), jnp.float32)
    two_tiles = jax.ShapeDtypeStruct((2 * rows, frames), jnp.float32)
    work = 2 * rows * frames * pix_dev
    block_bytes = 2 * frames * pix_dev

    near_a = send(intensity[:, :half], plan.shift)
    near_b = send(intensity[:, half:], plan.shift)
    own = vmem_call(own_kernel, tile_sums, [whole, whole], "own", work, block_bytes)(intensity, labels)
    far_a = send(near_a, plan.relay)
    held, _ = lax.optimization_barrier((intensity, near_a))
    ends = send(held, plan.ends)
    far_b = send(near_b, plan.relay)

    core_send, core_keep = vmem_call(
        near_kernel, [tile_sums, tile_sums], [scalars, whole, whole, whole, whole, whole], "near", work, 2 * block_bytes
    )(picks[:1], intensity, labels, near_a, near_b, own)
    core_got = send(core_send, plan.core)
    stays, near_side = picks[0] == 1, picks[1] == 1
    sums = core_keep[rows:] + core_got[rows:]
    kept, got = core_keep[:rows], core_got[:rows]
    mine = jnp.where(stays, kept + got, kept)
    theirs = jnp.where(stays, 0.0, got)
    side_keep = jnp.where(near_side, mine, theirs)
    side_send = jnp.concatenate([jnp.where(near_side, theirs, mine), sums], axis=0)
    side_got = send(side_send, plan.side)
    early = side_keep + side_got[:rows]
    sums = sums + side_got[rows:]
    swapped = send(sums, plan.swap)

    far = vmem_call(
        far_first_kernel, two_tiles, [left, left, left_labels, whole], "far_first", work, 2 * block_bytes
    )(intensity, ends, labels, far_a)
    late = plan.late()
    *outs, keep = vmem_call(
        far_second_kernel,
        [tile] * (len(late) + 1),
        [scalars, right, right, right_labels, whole, whole, whole],
        "far_second",
        work,
        2 * block_bytes,
        [pltpu.VMEM((3, rows, frames), jnp.float32)],
    )(picks[4:], intensity, ends, labels, far_b, far, early)
    got = []
    for slot, out in zip(late, outs):
        pairs = [(plan.index(s), plan.index(t)) for s, (t, _) in slot.items()]
        got.append(lax.ppermute(out, line, pairs))
    return vmem_call(
        functools.partial(final_kernel, pix_total),
        jax.ShapeDtypeStruct((CYCLES, frames, frames), jnp.float32),
        [scalars] + [whole] * 8,
        "final",
        rows * frames,
        8 * 4 * rows * frames,
    )(picks[2:3], early, keep, *got, sums, swapped)


def ring_body(intensity, cycle_labels):
    frames_dev, pix_dev = intensity.shape
    pix_total = pix_dev * lax.axis_size("pix")
    cycles = jnp.arange(CYCLES, dtype=cycle_labels.dtype)
    keep = cycle_labels[None, :] == cycles[:, None]
    grouped = jnp.where(keep[:, None, :], intensity[None], 0)
    local_sums = jnp.sum(grouped, axis=2, dtype=jnp.float32)
    cycle_sum = lax.psum(local_sums, "pix")
    frame_sums = lax.all_gather(cycle_sum, "tm", axis=1, tiled=True)
    blocks_count = lax.axis_size("tm")
    frames = frames_dev * blocks_count
    myself = lax.axis_index("tm")
    pairs = [(source, (source + 1) % blocks_count) for source in range(blocks_count)]

    def place(row, block, source):
        tile = jnp.einsum("qap,bp->qab", grouped, block, preferred_element_type=jnp.float32)
        return lax.dynamic_update_slice(row, tile, (0, 0, source * frames_dev))

    def turn(step, carry):
        block, row_now = carry
        row_now = place(row_now, block, (myself - step) % blocks_count)
        return (lax.ppermute(block, "tm", pairs), row_now)

    row = jnp.zeros((CYCLES, frames_dev, frames), jnp.float32)
    block, row = lax.fori_loop(0, blocks_count - 1, turn, (intensity, row))
    row = place(row, block, (myself + 1) % blocks_count)
    columns = frames // lax.axis_size("pix")
    start = lax.axis_index("pix") * columns
    gram = lax.psum_scatter(row, "pix", scatter_dimension=2, tiled=True)
    column_sums = lax.dynamic_slice_in_dim(frame_sums, start, columns, 1)
    return (pix_total // CYCLES) * gram / (cycle_sum[:, :, None] * column_sums[:, None, :])


def solution(mesh):
    placed = (P(("win", "tm"), "pix"), P("pix"))
    body = planned_body if mesh.shape["tm"] == 4 and mesh.shape["pix"] == 4 else ring_body
    return jax.shard_map(
        body, mesh=mesh, in_specs=placed, out_specs=P("win", "tm", "pix"), check_vma=False
    )
```

```python
import functools

import jax
import jax.numpy as jnp
import numpy as np
from jax import lax
from jax.experimental import pallas as pl
from jax.experimental.pallas import tpu as pltpu
from jax.sharding import PartitionSpec as P


CYCLES = 2
SUM_ROWS = 16
TILE, ENDS, EARLY = 0, 1, 2
STAYS, NEAR_SIDE, ALONE, DIAGONAL, HUB, FAR_END, KEEP, PICKS, REAL, WIDTH = 0, 1, 2, 3, 4, 5, 6, 7, 11, 15
CONTRACT_LAST = (((1,), (1,)), ((), ()))


def masks_of(labels, rows):
    cycle = lax.broadcasted_iota(jnp.int32, (rows, labels.shape[-1]), 0)
    return (cycle == labels).astype(jnp.float32).astype(jnp.bfloat16)


def masked(block, masks):
    return [block * masks[q : q + 1, :] for q in range(CYCLES)]


def products(left, right):
    return lax.dot_general(left, right, CONTRACT_LAST, preferred_element_type=jnp.float32)


def own_kernel(x_ref, labels_ref, out_ref):
    x = x_ref[...]
    masks = masks_of(labels_ref[...], SUM_ROWS)
    left = jnp.concatenate(masked(x, masks) + [masks], axis=0)
    out_ref[...] = products(left, x)


def cut_kernel(x_ref, out_ref):
    out_ref[...] = x_ref[...]


def near_kernel(pick_ref, x_ref, labels_ref, first_ref, second_ref, own_ref, send_ref, keep_ref):
    x = x_ref[...]
    half = first_ref.shape[1]
    rows = CYCLES * x.shape[0]
    left = jnp.concatenate(masked(x, masks_of(labels_ref[...], SUM_ROWS)), axis=0)
    near = products(left[:, :half], first_ref[...]) + products(left[:, half:], second_ref[...])
    own = own_ref[:rows, :]
    stays = pick_ref[STAYS] == 1
    send_ref[:rows, :] = jnp.where(stays, near, own)
    keep_ref[:rows, :] = jnp.where(stays, own, near)
    send_ref[rows:, :] = own_ref[rows:, :]
    keep_ref[rows:, :] = own_ref[rows:, :]


def far_products(pick_ref, x_ref, labels_ref, inner_ref, outer_ref):
    masks = masks_of(labels_ref[...], SUM_ROWS)
    outer = outer_ref[...]
    left = jnp.concatenate(masked(x_ref[...], masks) + masked(outer, masks), axis=0)
    return products(left, jnp.where(pick_ref[HUB] == 1, inner_ref[...], outer))


def far_first_kernel(pick_ref, x_ref, labels_ref, inner_ref, outer_ref, out_ref):
    out_ref[...] = far_products(pick_ref, x_ref, labels_ref, inner_ref, outer_ref)


def far_second_kernel(pick_ref, x_ref, labels_ref, inner_ref, outer_ref, sofar_ref, early_ref, *rest):
    outs, keep_ref, tiles = rest[:-2], rest[-2], rest[-1]
    rows = early_ref.shape[0]
    far = sofar_ref[...] + far_products(pick_ref, x_ref, labels_ref, inner_ref, outer_ref)
    tiles[TILE] = far[:rows, :]
    tiles[ENDS] = far[rows:, :]
    tiles[EARLY] = early_ref[...]
    keep_ref[...] = jnp.where(pick_ref[KEEP] == 1, far[:rows, :], 0.0)
    for slot, out_ref in enumerate(outs):
        out_ref[...] = tiles[pick_ref[PICKS + slot]]


def final_kernel(pix_total, pick_ref, early_ref, keep_ref, a_ref, b_ref, c_ref, d_ref, sums_ref, swapped_ref, out_ref):
    frames = out_ref.shape[1]
    sums = sums_ref[...]
    columns = jnp.where(pick_ref[DIAGONAL] == 1, sums, swapped_ref[...])

    def arrived(slot, ref, part):
        return jnp.where(pick_ref[REAL + slot] == 1, ref[part, :], 0.0)

    for q in range(CYCLES):
        part = slice(q * frames, (q + 1) * frames)
        turned = arrived(0, a_ref, part) + arrived(1, b_ref, part)
        gram = early_ref[part, :] + keep_ref[part, :] + arrived(2, c_ref, part) + arrived(3, d_ref, part) + turned.T
        row_sum = jnp.broadcast_to(sums[q : q + 1, :], (frames, frames)).T
        out_ref[q] = (pix_total // CYCLES) * gram / (row_sum * columns[q : q + 1, :])


def vmem_call(kernel, out_shapes, in_specs, flops, bytes_accessed, scratch=()):
    many = isinstance(out_shapes, (list, tuple))
    whole = pl.BlockSpec(memory_space=pltpu.VMEM)
    return pl.pallas_call(
        kernel,
        out_shape=out_shapes,
        grid=(1,),
        in_specs=in_specs,
        out_specs=[whole] * len(out_shapes) if many else whole,
        scratch_shapes=scratch,
        compiler_params=pltpu.CompilerParams(vmem_limit_bytes=24 * 2**20),
        cost_estimate=pl.CostEstimate(flops=flops, bytes_accessed=bytes_accessed, transcendentals=0),
    )


def completed(count, edges, cost):
    target_of = dict(edges)
    free = [s for s in range(count) if s not in target_of]
    open_targets = [t for t in range(count) if t not in set(target_of.values())]
    size = len(free)
    price = [[cost(s, t) for t in open_targets] for s in free]
    row_cost, column_cost = [0] * (size + 1), [0] * (size + 1)
    owner, back = [0] * (size + 1), [0] * (size + 1)
    for row in range(1, size + 1):
        owner[0], column = row, 0
        least, done = [float("inf")] * (size + 1), [False] * (size + 1)
        while owner[column]:
            done[column] = True
            here, step, following = owner[column], float("inf"), 0
            for j in range(1, size + 1):
                if not done[j]:
                    value = price[here - 1][j - 1] - row_cost[here] - column_cost[j]
                    if value < least[j]:
                        least[j], back[j] = value, column
                    if least[j] < step:
                        step, following = least[j], j
            for j in range(size + 1):
                if done[j]:
                    row_cost[owner[j]] += step
                    column_cost[j] -= step
                else:
                    least[j] -= step
            column = following
        while column:
            owner[column] = owner[back[column]]
            column = back[column]
    for j in range(1, size + 1):
        target_of[free[owner[j] - 1]] = open_targets[j - 1]
    return sorted(target_of.items())


class Plan:
    def __init__(self, blocks):
        self.last = blocks - 1
        self.devices = [(z, x, c) for z in range(blocks) for x in range(2) for c in range(2)]

    def index(self, place):
        z, x, c = place
        return z * 4 + x * 2 + c

    def pairs(self, rule):
        return [(self.index(place), self.index(rule(*place))) for place in self.devices]

    def shift(self, z, x, c):
        t = z + 1 - 2 * c
        return (t, x, c) if 0 <= t <= self.last else (z, x, 1 - c)

    def hub(self, z, c):
        return z == 2 - c

    def far_end(self, z, c):
        return z == (self.last if c == 0 else 0)

    def inner(self, z, x, c):
        return (2 - c, x, c) if z == 1 + c else (z, x, 1 - c)

    def outer(self, z, x, c):
        if self.hub(z, c):
            return (z + 1 - 2 * c, x, c)
        if self.far_end(z, c):
            return (z - 1 + 2 * c, x, c)
        return (z, 1 - x, c)

    def core(self, z, x, c):
        return (z, x, 1 - c)

    def side(self, z, x, c):
        return (z, 1 - x, c)

    def swap(self, z, x, c):
        if 2 * x + c == z:
            t = z ^ 1
            return (t, t // 2, t % 2)
        return (2 * x + c, z // 2, z % 2)

    def late(self):
        a, b, c, d = (2, 0, 0), (2, 1, 0), (0, 0, 1), (0, 1, 1)
        lower, upper = (0, 1, 0), (2, 0, 0)
        corner, other = (0, 1, 1), (3, 0, 0)
        slots = [
            {b: (lower, TILE), c: (upper, TILE), a: (corner, ENDS)},
            {a: (lower, TILE), d: (upper, TILE), b: (corner, ENDS)},
            {b: (upper, TILE), c: (lower, TILE), a: (other, ENDS)},
            {d: (lower, TILE), b: (other, ENDS)},
        ]

        def mirror(place):
            z, x, k = place
            return (self.last - z, 1 - x, 1 - k)

        full = []
        for slot in slots:
            both = dict(slot)
            for source, (target, tile) in slot.items():
                both[mirror(source)] = (mirror(target), tile)
            full.append(both)
        for place in self.devices:
            z, x, c = place
            if abs(2 * x + c - z) == 1:
                full[1][place] = (self.swap(*place), EARLY)
        return full

    def late_pairs(self, slot):
        def cost(source, target):
            if source == target:
                return 1000
            (z, x, c), (tz, tx, tc) = self.devices[source], self.devices[target]
            return 20 * abs(z - tz) + 5 * (x != tx) + (c != tc)

        edges = [(self.index(source), self.index(target)) for source, (target, _) in slot.items()]
        return completed(len(self.devices), edges, cost)

    def table(self):
        late = self.late()
        rows = []
        for place in self.devices:
            z, x, c = place
            stays = z % 2 == c
            row = [0] * WIDTH
            row[STAYS] = stays
            row[NEAR_SIDE] = x == z // 2
            row[ALONE] = stays or z in (0, self.last)
            row[DIAGONAL] = 2 * x + c == z
            row[HUB] = self.hub(z, c)
            row[FAR_END] = self.far_end(z, c)
            row[KEEP] = place in ((2, 0, 0), (1, 1, 1))
            for k, slot in enumerate(late):
                row[PICKS + k] = slot[place][1] if place in slot else TILE
                row[REAL + k] = place in [target for target, _ in slot.values()]
            rows.append(row)
        return np.asarray(rows, np.int32)


def planned_body(intensity, cycle_labels):
    frames, pix_dev = intensity.shape
    half = pix_dev // 2
    pix_total = pix_dev * lax.axis_size("pix")
    plan = Plan(lax.axis_size("tm"))
    line = ("tm", "pix")

    def send(value, pairs):
        return lax.ppermute(value, line, pairs)

    labels = cycle_labels.reshape(1, pix_dev)
    whole = pl.BlockSpec(memory_space=pltpu.VMEM)
    scalars = pl.BlockSpec(memory_space=pltpu.SMEM)
    halves = [pl.BlockSpec((frames, half), lambda step, k=k: (0, k)) for k in range(2)]
    half_labels = [pl.BlockSpec((1, half), lambda step, k=k: (0, k)) for k in range(2)]
    rows = CYCLES * frames
    tile = jax.ShapeDtypeStruct((rows, frames), jnp.float32)
    tile_sums = jax.ShapeDtypeStruct((rows + SUM_ROWS, frames), jnp.float32)
    two_tiles = jax.ShapeDtypeStruct((2 * rows, frames), jnp.float32)
    piece = jax.ShapeDtypeStruct((frames, half), intensity.dtype)
    work = 2 * rows * frames * pix_dev
    block_bytes = 2 * frames * pix_dev

    shift = plan.pairs(plan.shift)
    pieces, near = [], []
    for k in range(2):
        cut = vmem_call(cut_kernel, piece, [halves[k]], 0, block_bytes)(intensity)
        pieces.append(cut)
        near.append(send(cut, shift))
    picks = jnp.asarray(plan.table())[lax.axis_index(line)]
    own = vmem_call(own_kernel, tile_sums, [whole, whole], work, block_bytes)(intensity, labels)
    inner, outer = [], []
    for k in range(2):
        inner.append(send(near[k], plan.pairs(plan.inner)))
        chosen = jnp.where(picks[FAR_END] == 1, pieces[k], near[k])
        outer.append(send(chosen, plan.pairs(plan.outer)))

    core_send, core_keep = vmem_call(
        near_kernel, [tile_sums, tile_sums], [scalars] + [whole] * 5, work, 2 * block_bytes
    )(picks, intensity, labels, *near, own)
    core_got = send(core_send, plan.pairs(plan.core))
    near_side = picks[NEAR_SIDE] == 1
    sums = core_keep[rows:] + core_got[rows:]
    kept, got = core_keep[:rows], core_got[:rows]
    mine = jnp.where(picks[STAYS] == 1, kept + got, kept)
    theirs = jnp.where(picks[ALONE] == 1, 0.0, got)
    side_keep = jnp.where(near_side, mine, theirs)
    side_send = jnp.concatenate([jnp.where(near_side, theirs, mine), sums], axis=0)
    side_got = send(side_send, plan.pairs(plan.side))
    early = side_keep + side_got[:rows]
    sums = sums + side_got[rows:]
    swapped = send(sums, plan.pairs(plan.swap))

    far_specs = [[scalars, halves[k], half_labels[k], whole, whole] for k in range(2)]
    far = vmem_call(far_first_kernel, two_tiles, far_specs[0], work, 2 * block_bytes)(
        picks, intensity, labels, inner[0], outer[0]
    )
    late = plan.late()
    *outs, keep = vmem_call(
        far_second_kernel,
        [tile] * (len(late) + 1),
        far_specs[1] + [whole, whole],
        work,
        2 * block_bytes,
        [pltpu.VMEM((3, rows, frames), jnp.float32)],
    )(picks, intensity, labels, inner[1], outer[1], far, early)
    got = [send(out, plan.late_pairs(slot)) for slot, out in zip(late, outs)]
    return vmem_call(
        functools.partial(final_kernel, pix_total),
        jax.ShapeDtypeStruct((CYCLES, frames, frames), jnp.float32),
        [scalars] + [whole] * 8,
        rows * frames,
        8 * 4 * rows * frames,
    )(picks, early, keep, *got, sums, swapped)


def ring_body(intensity, cycle_labels):
    frames_dev, pix_dev = intensity.shape
    pix_total = pix_dev * lax.axis_size("pix")
    cycles = jnp.arange(CYCLES, dtype=cycle_labels.dtype)
    keep = cycle_labels[None, :] == cycles[:, None]
    grouped = jnp.where(keep[:, None, :], intensity[None], 0)
    local_sums = jnp.sum(grouped, axis=2, dtype=jnp.float32)
    cycle_sum = lax.psum(local_sums, "pix")
    frame_sums = lax.all_gather(cycle_sum, "tm", axis=1, tiled=True)
    blocks_count = lax.axis_size("tm")
    frames = frames_dev * blocks_count
    myself = lax.axis_index("tm")
    pairs = [(source, (source + 1) % blocks_count) for source in range(blocks_count)]

    def place(row, block, source):
        tile = jnp.einsum("qap,bp->qab", grouped, block, preferred_element_type=jnp.float32)
        return lax.dynamic_update_slice(row, tile, (0, 0, source * frames_dev))

    def turn(step, carry):
        block, row_now = carry
        row_now = place(row_now, block, (myself - step) % blocks_count)
        return (lax.ppermute(block, "tm", pairs), row_now)

    row = jnp.zeros((CYCLES, frames_dev, frames), jnp.float32)
    block, row = lax.fori_loop(0, blocks_count - 1, turn, (intensity, row))
    row = place(row, block, (myself + 1) % blocks_count)
    columns = frames // lax.axis_size("pix")
    start = lax.axis_index("pix") * columns
    gram = lax.psum_scatter(row, "pix", scatter_dimension=2, tiled=True)
    column_sums = lax.dynamic_slice_in_dim(frame_sums, start, columns, 1)
    return (pix_total // CYCLES) * gram / (cycle_sum[:, :, None] * column_sums[:, None, :])


def solution(mesh):
    placed = (P(("win", "tm"), "pix"), P("pix"))
    planned = mesh.shape["tm"] == 4 and mesh.shape["pix"] == 4

    def body(intensity, cycle_labels):
        return (planned_body if planned else ring_body)(intensity, cycle_labels)

    return jax.shard_map(body, mesh=mesh, in_specs=placed, out_specs=P("win", "tm", "pix"), check_vma=False)
```

```python
import functools

import jax
import jax.numpy as jnp
from jax import lax
from jax.experimental import pallas as pl
from jax.experimental.pallas import tpu as pltpu
from jax.sharding import PartitionSpec as P


CYCLES = 2
SUM_ROWS = 16
TILE, ENDS, EARLY = 0, 1, 2
LINE = ("win", "tm", "pix")
CONTRACT_LAST = (((1,), (1,)), ((), ()))


def masks_of(labels, rows):
    cycle = lax.broadcasted_iota(jnp.int32, (rows, labels.shape[-1]), 0)
    return (cycle == labels).astype(jnp.float32).astype(jnp.bfloat16)


def masked(block, masks):
    return [block * masks[q : q + 1, :] for q in range(CYCLES)]


def products(left, right):
    return lax.dot_general(left, right, CONTRACT_LAST, preferred_element_type=jnp.float32)


def chosen(mask, value_if, value_else):
    return jnp.where(bit(mask) == 1, value_if, value_else)


def bit(mask):
    place = lax.axis_index("tm") * lax.axis_size("pix") + lax.axis_index("pix")
    return (jnp.int32(mask) >> place) & 1


def cut_kernel(k, x_ref, out_ref, sem):
    half = out_ref.shape[1]
    copy = pltpu.make_async_copy(x_ref.at[:, k * half : (k + 1) * half], out_ref, sem)
    copy.start()
    copy.wait()


def pick_kernel(mask, if_ref, else_ref, out_ref):
    out_ref[...] = chosen(mask, if_ref[...], else_ref[...])


def early_kernel(near_side, beside, mine_ref, theirs_ref, passed_ref, out_ref):
    total = chosen(near_side, mine_ref[...], theirs_ref[...]) + passed_ref[...]
    out_ref[...] = chosen(beside, total, 0.0)


def own_kernel(first_ref, second_ref, labels_ref, out_ref):
    masks = masks_of(labels_ref[...], SUM_ROWS)
    half = first_ref.shape[1]
    total = None
    for k, ref in enumerate((first_ref, second_ref)):
        x, here = ref[...], masks[:, k * half : (k + 1) * half]
        part = products(jnp.concatenate(masked(x, here) + [here], axis=0), x)
        total = part if total is None else total + part
    out_ref[...] = total


def near_kernel(first_ref, second_ref, labels_ref, near_first_ref, near_second_ref, out_ref):
    masks = masks_of(labels_ref[...], SUM_ROWS)
    half = first_ref.shape[1]
    total = None
    for k, (ref, near_ref) in enumerate(((first_ref, near_first_ref), (second_ref, near_second_ref))):
        part = products(jnp.concatenate(masked(ref[...], masks[:, k * half : (k + 1) * half]), axis=0), near_ref[...])
        total = part if total is None else total + part
    out_ref[...] = total


def far_products(hub, x_ref, labels_ref, inner_ref, outer_ref):
    masks = masks_of(labels_ref[...], SUM_ROWS)
    outer = outer_ref[...]
    left = jnp.concatenate(masked(x_ref[...], masks) + masked(outer, masks), axis=0)
    return products(left, chosen(hub, inner_ref[...], outer))


def far_first_kernel(hub, x_ref, labels_ref, inner_ref, outer_ref, out_ref):
    out_ref[...] = far_products(hub, x_ref, labels_ref, inner_ref, outer_ref)


def far_second_kernel(roles, x_ref, labels_ref, inner_ref, outer_ref, sofar_ref, *rest):
    outs, last_ref, keep_ref = rest[:-2], rest[-2], rest[-1]
    rows = keep_ref.shape[0]
    far = sofar_ref[...] + far_products(roles["hub"], x_ref, labels_ref, inner_ref, outer_ref)
    tile, ends = far[:rows, :], far[rows:, :]
    keep_ref[...] = chosen(roles["keep"], tile, 0.0)
    for slot, out_ref in enumerate(outs + (last_ref,)):
        out_ref[...] = chosen(roles["ends"][slot], ends, tile)


def final_kernel(pix_total, roles, keep_ref, early_ref, own_ref, a_ref, b_ref, c_ref, d_ref, sums_ref, swapped_ref, out_ref):
    frames = out_ref.shape[1]
    sums = sums_ref[...]
    columns = chosen(roles["diagonal"], sums, swapped_ref[...])

    def arrived(mask, ref, part):
        return chosen(mask, ref[part, :], 0.0)

    for q in range(CYCLES):
        part = slice(q * frames, (q + 1) * frames)
        turned = arrived(roles["real"][0], a_ref, part) + arrived(roles["real"][1], b_ref, part)
        turned = turned + arrived(roles["beside"], d_ref, part)
        gram = keep_ref[part, :] + early_ref[part, :] + arrived(roles["diagonal"], own_ref, part)
        gram = gram + arrived(roles["real"][2], c_ref, part) + arrived(roles["real"][3], d_ref, part) + turned.T
        row_sum = jnp.broadcast_to(sums[q : q + 1, :], (frames, frames)).T
        out_ref[q] = (pix_total // CYCLES) * gram / (row_sum * columns[q : q + 1, :])


def vmem_call(kernel, out_shapes, in_specs, flops, bytes_accessed, scratch=(), limit=16 * 2**20):
    many = isinstance(out_shapes, (list, tuple))
    whole = pl.BlockSpec(memory_space=pltpu.VMEM)
    return pl.pallas_call(
        kernel,
        out_shape=out_shapes,
        grid=(1,),
        in_specs=in_specs,
        out_specs=[whole] * len(out_shapes) if many else whole,
        scratch_shapes=scratch,
        compiler_params=pltpu.CompilerParams(vmem_limit_bytes=limit),
        cost_estimate=pl.CostEstimate(flops=flops, bytes_accessed=bytes_accessed, transcendentals=0),
    )


def completed(count, edges, cost):
    target_of = dict(edges)
    free = [s for s in range(count) if s not in target_of]
    open_targets = [t for t in range(count) if t not in set(target_of.values())]
    size = len(free)
    price = [[cost(s, t) for t in open_targets] for s in free]
    row_cost, column_cost = [0] * (size + 1), [0] * (size + 1)
    owner, back = [0] * (size + 1), [0] * (size + 1)
    for row in range(1, size + 1):
        owner[0], column = row, 0
        least, done = [float("inf")] * (size + 1), [False] * (size + 1)
        while owner[column]:
            done[column] = True
            here, step, following = owner[column], float("inf"), 0
            for j in range(1, size + 1):
                if not done[j]:
                    value = price[here - 1][j - 1] - row_cost[here] - column_cost[j]
                    if value < least[j]:
                        least[j], back[j] = value, column
                    if least[j] < step:
                        step, following = least[j], j
            for j in range(size + 1):
                if done[j]:
                    row_cost[owner[j]] += step
                    column_cost[j] -= step
                else:
                    least[j] -= step
            column = following
        while column:
            owner[column] = owner[back[column]]
            column = back[column]
    for j in range(1, size + 1):
        target_of[free[owner[j] - 1]] = open_targets[j - 1]
    return sorted(target_of.items())


class Plan:
    def __init__(self, windows, blocks):
        self.windows = windows
        self.last = blocks - 1
        self.places = [(z, x, c) for z in range(blocks) for x in range(2) for c in range(2)]
        self.devices = [(w,) + place for w in range(windows) for place in self.places]

    def index(self, device):
        return self.devices.index(device)

    def pairs(self, rule):
        found = []
        for device in self.devices:
            place = rule(*device[1:])
            target = (device[0] ^ 1,) + device[1:] if place is None else (device[0],) + place
            found.append((self.index(device), self.index(target)))
        return found

    def mask(self, rule):
        return sum(1 << k for k, place in enumerate(self.places) if rule(*place))

    def shift(self, z, x, c):
        t = z + 1 - 2 * c
        return (t, x, c) if 0 <= t <= self.last else (z, x, 1 - c)

    def hub(self, z, x, c):
        return z == 2 - c

    def far_end(self, z, x, c):
        return z == (self.last if c == 0 else 0)

    def inner(self, z, x, c):
        return (2 - c, x, c) if z == 1 + c else (z, x, 1 - c)

    def outer(self, z, x, c):
        if self.hub(z, x, c):
            return (z + 1 - 2 * c, x, c)
        if self.far_end(z, x, c):
            return (z - 1 + 2 * c, x, c)
        return None

    def core(self, z, x, c):
        return (z, x, 1 - c)

    def side(self, z, x, c):
        return (z, 1 - x, c)

    def near_side(self, z, x, c):
        return (z, 1 - x, c)

    def swap(self, z, x, c):
        return None if 2 * x + c == z else (2 * x + c, z // 2, z % 2)

    def late(self):
        a, b, c, d = (2, 0, 0), (2, 1, 0), (0, 0, 1), (0, 1, 1)
        lower, upper = (0, 1, 0), (2, 0, 0)
        corner, other = (0, 1, 1), (3, 0, 0)
        slots = [
            {b: (lower, TILE), c: (upper, TILE), a: (corner, ENDS)},
            {a: (lower, TILE), d: (upper, TILE), b: (corner, ENDS)},
            {b: (upper, TILE), c: (lower, TILE), a: (other, ENDS)},
            {d: (lower, TILE), b: (other, ENDS)},
        ]

        def mirror(place):
            z, x, k = place
            return (self.last - z, 1 - x, 1 - k)

        full = []
        for slot in slots:
            both = dict(slot)
            for source, (target, tile) in slot.items():
                both[mirror(source)] = (mirror(target), tile)
            full.append(both)
        for place in self.places:
            z, x, c = place
            if abs(2 * x + c - z) == 1:
                full[-1][place] = (self.swap(*place), EARLY)
        return full

    def late_pairs(self, slot):
        def cost(source, target):
            if source == target:
                return 1000
            (w, z, x, c), (tw, tz, tx, tc) = self.devices[source], self.devices[target]
            return 20 * abs(z - tz) + 6 * (x != tx) + 5 * (w != tw) + (c != tc)

        edges = [
            (self.index((w,) + source), self.index((w,) + target))
            for w in range(self.windows)
            for source, (target, _) in slot.items()
        ]
        return completed(len(self.devices), edges, cost)

    def roles(self):
        late = self.late()

        def picks(slot, value):
            return self.mask(lambda *place: place in slot and slot[place][1] == value)

        return {
            "hub": self.mask(self.hub),
            "keep": self.mask(lambda *place: place in ((2, 0, 0), (1, 1, 1))),
            "diagonal": self.mask(lambda z, x, c: 2 * x + c == z),
            "beside": self.mask(lambda z, x, c: abs(2 * x + c - z) == 1),
            "ends": [picks(slot, ENDS) for slot in late],
            "early": picks(late[-1], EARLY),
            "real": [
                self.mask(lambda *place: place in [t for t, kind in slot.values() if kind != EARLY]) for slot in late
            ],
        }


def planned_body(intensity, cycle_labels):
    frames, pix_dev = intensity.shape
    half = pix_dev // 2
    pix_total = pix_dev * lax.axis_size("pix")
    plan = Plan(lax.axis_size("win"), lax.axis_size("tm"))
    roles = plan.roles()

    def send(value, pairs):
        return lax.ppermute(value, LINE, pairs)

    def call(kernel, shapes, specs, *args, **options):
        return vmem_call(kernel, shapes, specs, work, block_bytes, **options)(*args)

    labels = cycle_labels.reshape(1, pix_dev)
    whole = pl.BlockSpec(memory_space=pltpu.VMEM)
    half_labels = [pl.BlockSpec((1, half), lambda step, k=k: (0, k)) for k in range(2)]
    rows = CYCLES * frames
    tile = jax.ShapeDtypeStruct((rows, frames), jnp.float32)
    tile_sums = jax.ShapeDtypeStruct((rows + SUM_ROWS, frames), jnp.float32)
    two_tiles = jax.ShapeDtypeStruct((2 * rows, frames), jnp.float32)
    piece = jax.ShapeDtypeStruct((frames, half), intensity.dtype)
    work = 2 * rows * frames * pix_dev
    block_bytes = 2 * frames * pix_dev

    held = pltpu.with_memory_space_constraint(intensity, pltpu.HBM)
    pieces, near = [], []
    for k in range(2):
        cut = functools.partial(cut_kernel, k)
        in_hbm = pl.BlockSpec(memory_space=pltpu.HBM)
        pieces.append(call(cut, piece, [in_hbm], held, scratch=[pltpu.SemaphoreType.DMA]))
        near.append(send(pieces[k], plan.pairs(plan.shift)))

    own = call(own_kernel, tile_sums, [whole] * 3, *pieces, labels)
    own = own + send(own, plan.pairs(plan.core))
    own = own + send(own, plan.pairs(plan.side))
    sums = own[rows:]

    inner, outer = [], []
    for k in range(2):
        inner.append(send(near[k], plan.pairs(plan.inner)))
        passed = call(functools.partial(pick_kernel, plan.mask(plan.far_end)), piece, [whole] * 2, pieces[k], near[k])
        outer.append(send(passed, plan.pairs(plan.outer)))

    mine = call(near_kernel, tile, [whole] * 5, *pieces, labels, *near)
    theirs = send(mine, plan.pairs(plan.core))
    near_side = plan.mask(lambda z, x, c: x == z // 2)
    passed = call(functools.partial(pick_kernel, near_side), tile, [whole] * 2, theirs, mine)
    passed = send(passed, plan.pairs(plan.near_side))
    early = call(functools.partial(early_kernel, near_side, roles["beside"]), tile, [whole] * 3, mine, theirs, passed)
    swapped = send(sums, plan.pairs(plan.swap))

    far_specs = [[whole, half_labels[k], whole, whole] for k in range(2)]
    far = call(
        functools.partial(far_first_kernel, roles["hub"]), two_tiles, far_specs[0],
        pieces[0], labels, inner[0], outer[0],
    )
    late = plan.late()
    *outs, keep = call(
        functools.partial(far_second_kernel, roles), [tile] * (len(late) + 1), far_specs[1] + [whole],
        pieces[1], labels, inner[1], outer[1], far,
    )
    outs[-1] = call(functools.partial(pick_kernel, roles["early"]), tile, [whole] * 2, early, outs[-1])
    got = [send(out, plan.late_pairs(slot)) for slot, out in zip(late, outs)]
    return call(
        functools.partial(final_kernel, pix_total, roles),
        jax.ShapeDtypeStruct((CYCLES, frames, frames), jnp.float32), [whole] * 9,
        keep, early, own, *got, sums, swapped,
    )


def ring_body(intensity, cycle_labels):
    frames_dev, pix_dev = intensity.shape
    pix_total = pix_dev * lax.axis_size("pix")
    cycles = jnp.arange(CYCLES, dtype=cycle_labels.dtype)
    keep = cycle_labels[None, :] == cycles[:, None]
    grouped = jnp.where(keep[:, None, :], intensity[None], 0)
    local_sums = jnp.sum(grouped, axis=2, dtype=jnp.float32)
    cycle_sum = lax.psum(local_sums, "pix")
    frame_sums = lax.all_gather(cycle_sum, "tm", axis=1, tiled=True)
    blocks_count = lax.axis_size("tm")
    frames = frames_dev * blocks_count
    myself = lax.axis_index("tm")
    pairs = [(source, (source + 1) % blocks_count) for source in range(blocks_count)]

    def place(row, block, source):
        tile = jnp.einsum("qap,bp->qab", grouped, block, preferred_element_type=jnp.float32)
        return lax.dynamic_update_slice(row, tile, (0, 0, source * frames_dev))

    def turn(step, carry):
        block, row_now = carry
        row_now = place(row_now, block, (myself - step) % blocks_count)
        return (lax.ppermute(block, "tm", pairs), row_now)

    row = jnp.zeros((CYCLES, frames_dev, frames), jnp.float32)
    block, row = lax.fori_loop(0, blocks_count - 1, turn, (intensity, row))
    row = place(row, block, (myself + 1) % blocks_count)
    columns = frames // lax.axis_size("pix")
    start = lax.axis_index("pix") * columns
    gram = lax.psum_scatter(row, "pix", scatter_dimension=2, tiled=True)
    column_sums = lax.dynamic_slice_in_dim(frame_sums, start, columns, 1)
    return (pix_total // CYCLES) * gram / (cycle_sum[:, :, None] * column_sums[:, None, :])


def solution(mesh):
    placed = (P(("win", "tm"), "pix"), P("pix"))
    planned = mesh.shape["tm"] == 4 and mesh.shape["pix"] == 4 and mesh.shape["win"] % 2 == 0

    def body(intensity, cycle_labels):
        return (planned_body if planned else ring_body)(intensity, cycle_labels)

    return jax.shard_map(body, mesh=mesh, in_specs=placed, out_specs=P("win", "tm", "pix"), check_vma=False)
```

```python
import functools

import jax
import jax.numpy as jnp
from jax import lax
from jax.experimental import pallas as pl
from jax.experimental.pallas import tpu as pltpu
from jax.sharding import PartitionSpec as P


CYCLES = 2
SUM_ROWS = 16
TILE, ENDS, EARLY = 0, 1, 2
LINE = ("win", "tm", "pix")
CONTRACT_LAST = (((1,), (1,)), ((), ()))


def masks_of(labels, rows):
    cycle = lax.broadcasted_iota(jnp.int32, (rows, labels.shape[-1]), 0)
    return (cycle == labels).astype(jnp.float32).astype(jnp.bfloat16)


def masked(block, masks):
    return [block * masks[q : q + 1, :] for q in range(CYCLES)]


def products(left, right):
    return lax.dot_general(left, right, CONTRACT_LAST, preferred_element_type=jnp.float32)


def chosen(mask, value_if, value_else):
    return jnp.where(bit(mask) == 1, value_if, value_else)


def bit(mask):
    place = lax.axis_index("tm") * lax.axis_size("pix") + lax.axis_index("pix")
    return (jnp.int32(mask) >> place) & 1


def cut_kernel(k, x_ref, out_ref, sem):
    half = out_ref.shape[1]
    copy = pltpu.make_async_copy(x_ref.at[:, k * half : (k + 1) * half], out_ref, sem)
    copy.start()
    copy.wait()


def pick_kernel(mask, if_ref, else_ref, out_ref):
    out_ref[...] = chosen(mask, if_ref[...], else_ref[...])


def early_kernel(near_side, beside, mine_ref, theirs_ref, passed_ref, out_ref):
    total = chosen(near_side, mine_ref[...], theirs_ref[...]) + passed_ref[...]
    out_ref[...] = chosen(beside, total, 0.0)


def own_kernel(first_ref, second_ref, labels_ref, out_ref):
    masks = masks_of(labels_ref[...], SUM_ROWS)
    half = first_ref.shape[1]
    total = None
    for k, ref in enumerate((first_ref, second_ref)):
        x, here = ref[...], masks[:, k * half : (k + 1) * half]
        part = products(jnp.concatenate(masked(x, here) + [here], axis=0), x)
        total = part if total is None else total + part
    out_ref[...] = total


def near_kernel(first_ref, second_ref, labels_ref, near_first_ref, near_second_ref, out_ref):
    masks = masks_of(labels_ref[...], SUM_ROWS)
    half = first_ref.shape[1]
    total = None
    for k, (ref, near_ref) in enumerate(((first_ref, near_first_ref), (second_ref, near_second_ref))):
        part = products(jnp.concatenate(masked(ref[...], masks[:, k * half : (k + 1) * half]), axis=0), near_ref[...])
        total = part if total is None else total + part
    out_ref[...] = total


def far_products(hub, x_ref, labels_ref, inner_ref, outer_ref):
    masks = masks_of(labels_ref[...], SUM_ROWS)
    outer = outer_ref[...]
    met = chosen(hub, inner_ref[...], outer)
    return products(jnp.concatenate([x_ref[...], outer], axis=0), jnp.concatenate(masked(met, masks), axis=0))


def far_first_kernel(hub, x_ref, labels_ref, inner_ref, outer_ref, out_ref):
    out_ref[...] = far_products(hub, x_ref, labels_ref, inner_ref, outer_ref)


def far_second_kernel(roles, x_ref, labels_ref, inner_ref, outer_ref, sofar_ref, *rest):
    outs, keep_ref = rest[:-1], rest[-1]
    frames = x_ref.shape[0]
    far = sofar_ref[...] + far_products(roles["hub"], x_ref, labels_ref, inner_ref, outer_ref)
    for q in range(CYCLES):
        part = slice(q * frames, (q + 1) * frames)
        tile, ends = far[:frames, part], far[frames:, part]
        keep_ref[part, :] = chosen(roles["keep"], tile, 0.0)
        for slot, out_ref in enumerate(outs):
            out_ref[part, :] = chosen(roles["ends"][slot], ends, tile)


def final_kernel(pix_total, roles, keep_ref, early_ref, own_ref, a_ref, b_ref, c_ref, d_ref, sums_ref, swapped_ref, out_ref):
    frames = out_ref.shape[1]
    sums = sums_ref[...]
    columns = chosen(roles["diagonal"], sums, swapped_ref[...])

    def arrived(mask, ref, part):
        return chosen(mask, ref[part, :], 0.0)

    for q in range(CYCLES):
        part = slice(q * frames, (q + 1) * frames)
        turned = arrived(roles["real"][0], a_ref, part) + arrived(roles["real"][1], b_ref, part)
        gram = keep_ref[part, :] + early_ref[part, :] + arrived(roles["diagonal"], own_ref, part)
        gram = gram + arrived(roles["real"][2], c_ref, part) + arrived(roles["real"][3], d_ref, part) + turned.T
        row_sum = jnp.broadcast_to(sums[q : q + 1, :], (frames, frames)).T
        out_ref[q] = (pix_total // CYCLES) * gram / (row_sum * columns[q : q + 1, :])


def vmem_call(kernel, out_shapes, in_specs, flops, bytes_accessed, scratch=(), limit=16 * 2**20):
    many = isinstance(out_shapes, (list, tuple))
    whole = pl.BlockSpec(memory_space=pltpu.VMEM)
    return pl.pallas_call(
        kernel,
        out_shape=out_shapes,
        grid=(1,),
        in_specs=in_specs,
        out_specs=[whole] * len(out_shapes) if many else whole,
        scratch_shapes=scratch,
        compiler_params=pltpu.CompilerParams(vmem_limit_bytes=limit),
        cost_estimate=pl.CostEstimate(flops=flops, bytes_accessed=bytes_accessed, transcendentals=0),
    )


def completed(count, edges, cost):
    target_of = dict(edges)
    free = [s for s in range(count) if s not in target_of]
    open_targets = [t for t in range(count) if t not in set(target_of.values())]
    size = len(free)
    price = [[cost(s, t) for t in open_targets] for s in free]
    row_cost, column_cost = [0] * (size + 1), [0] * (size + 1)
    owner, back = [0] * (size + 1), [0] * (size + 1)
    for row in range(1, size + 1):
        owner[0], column = row, 0
        least, done = [float("inf")] * (size + 1), [False] * (size + 1)
        while owner[column]:
            done[column] = True
            here, step, following = owner[column], float("inf"), 0
            for j in range(1, size + 1):
                if not done[j]:
                    value = price[here - 1][j - 1] - row_cost[here] - column_cost[j]
                    if value < least[j]:
                        least[j], back[j] = value, column
                    if least[j] < step:
                        step, following = least[j], j
            for j in range(size + 1):
                if done[j]:
                    row_cost[owner[j]] += step
                    column_cost[j] -= step
                else:
                    least[j] -= step
            column = following
        while column:
            owner[column] = owner[back[column]]
            column = back[column]
    for j in range(1, size + 1):
        target_of[free[owner[j] - 1]] = open_targets[j - 1]
    return sorted(target_of.items())


class Plan:
    def __init__(self, windows, blocks):
        self.windows = windows
        self.last = blocks - 1
        self.places = [(z, x, c) for z in range(blocks) for x in range(2) for c in range(2)]
        self.devices = [(w,) + place for w in range(windows) for place in self.places]

    def index(self, device):
        return self.devices.index(device)

    def pairs(self, rule):
        found = []
        for device in self.devices:
            place = rule(*device[1:])
            target = (device[0] ^ 1,) + device[1:] if place is None else (device[0],) + place
            found.append((self.index(device), self.index(target)))
        return found

    def mask(self, rule):
        return sum(1 << k for k, place in enumerate(self.places) if rule(*place))

    def shift(self, z, x, c):
        t = z + 1 - 2 * c
        return (t, x, c) if 0 <= t <= self.last else (z, x, 1 - c)

    def hub(self, z, x, c):
        return z == 2 - c

    def far_end(self, z, x, c):
        return z == (self.last if c == 0 else 0)

    def inner(self, z, x, c):
        return (2 - c, x, c) if z == 1 + c else (z, x, 1 - c)

    def outer(self, z, x, c):
        if self.hub(z, x, c):
            return (z + 1 - 2 * c, x, c)
        if self.far_end(z, x, c):
            return (z - 1 + 2 * c, x, c)
        return None

    def core(self, z, x, c):
        return (z, x, 1 - c)

    def side(self, z, x, c):
        return (z, 1 - x, c)

    def cross(self, z, x, c):
        return (z, 1 - x, 1 - c if x == z // 2 else c)

    def swap(self, z, x, c):
        return None if 2 * x + c == z else (2 * x + c, z // 2, z % 2)

    def late(self):
        a, b, c, d = (2, 0, 0), (2, 1, 0), (0, 0, 1), (0, 1, 1)
        lower, upper = (0, 1, 0), (2, 0, 0)
        corner, other = (0, 1, 1), (3, 0, 0)
        slots = [
            {b: (lower, TILE), d: (upper, TILE), a: (corner, ENDS)},
            {a: (lower, TILE), c: (upper, TILE), b: (corner, ENDS)},
            {b: (upper, TILE), c: (lower, TILE), a: (other, ENDS)},
            {d: (lower, TILE), b: (other, ENDS)},
        ]

        def mirror(place):
            z, x, k = place
            return (self.last - z, 1 - x, 1 - k)

        full = []
        for slot in slots:
            both = dict(slot)
            for source, (target, tile) in slot.items():
                both[mirror(source)] = (mirror(target), tile)
            full.append(both)
        for place in self.places:
            z, x, c = place
            if abs(2 * x + c - z) == 1:
                full[0][place] = (self.swap(*place), EARLY)
        return full

    def links(self, source, target):
        (w, z, x, c), (tw, tz, tx, tc) = source, target
        step = 1 if tz > z else -1
        found = [("block", w, x, here, step) for here in range(z, tz, step)]
        if tx != x:
            found.append(("side", w, tz, x))
        if tw != w:
            found.append(("window", w, tz, tx))
        return found

    def late_pairs(self):
        load, slots = {}, []

        def carry(source, target):
            for link in self.links(source, target):
                load[link] = load.get(link, 0) + 1

        for slot in self.late():
            edges = [
                ((w,) + source, (w,) + target) for w in range(self.windows) for source, (target, _) in slot.items()
            ]
            for edge in edges:
                carry(*edge)
            slots.append([(self.index(source), self.index(target)) for source, target in edges])

        def cost(source, target):
            if source == target:
                return 10**6
            places = self.devices[source], self.devices[target]
            return 1 + sum(
                (20 if link[0] == "block" else 10) + 10 * load.get(link, 0) ** 2 for link in self.links(*places)
            )

        result = []
        for edges in slots:
            pairs = completed(len(self.devices), edges, cost)
            for source, target in set(pairs) - set(edges):
                carry(self.devices[source], self.devices[target])
            result.append(pairs)
        return result

    def roles(self):
        late = self.late()

        def picks(slot, value):
            return self.mask(lambda *place: place in slot and slot[place][1] == value)

        return {
            "hub": self.mask(self.hub),
            "keep": self.mask(lambda *place: place in ((2, 0, 0), (1, 1, 1))),
            "diagonal": self.mask(lambda z, x, c: 2 * x + c == z),
            "beside": self.mask(lambda z, x, c: abs(2 * x + c - z) == 1),
            "mine": self.mask(lambda z, x, c: x == z // 2),
            "ends": [picks(slot, ENDS) for slot in late],
            "early": picks(late[0], EARLY),
            "real": [self.mask(lambda *place: place in [t for t, _ in slot.values()]) for slot in late],
        }


def planned_body(intensity, cycle_labels):
    frames, pix_dev = intensity.shape
    half = pix_dev // 2
    pix_total = pix_dev * lax.axis_size("pix")
    plan = Plan(lax.axis_size("win"), lax.axis_size("tm"))
    roles = plan.roles()

    def send(value, pairs):
        return lax.ppermute(value, LINE, pairs)

    def call(kernel, shapes, specs, *args, **options):
        return vmem_call(kernel, shapes, specs, work, block_bytes, **options)(*args)

    labels = cycle_labels.reshape(1, pix_dev)
    whole = pl.BlockSpec(memory_space=pltpu.VMEM)
    half_labels = [pl.BlockSpec((1, half), lambda step, k=k: (0, k)) for k in range(2)]
    rows = CYCLES * frames
    tile = jax.ShapeDtypeStruct((rows, frames), jnp.float32)
    tile_sums = jax.ShapeDtypeStruct((rows + SUM_ROWS, frames), jnp.float32)
    two_tiles = jax.ShapeDtypeStruct((2 * frames, rows), jnp.float32)
    piece = jax.ShapeDtypeStruct((frames, half), intensity.dtype)
    work = 2 * rows * frames * pix_dev
    block_bytes = 2 * frames * pix_dev

    held = pltpu.with_memory_space_constraint(intensity, pltpu.HBM)
    pieces, near = [], []
    for k in range(2):
        cut = functools.partial(cut_kernel, k)
        in_hbm = pl.BlockSpec(memory_space=pltpu.HBM)
        pieces.append(call(cut, piece, [in_hbm], held, scratch=[pltpu.SemaphoreType.DMA]))
        near.append(send(pieces[k], plan.pairs(plan.shift)))

    own = call(own_kernel, tile_sums, [whole] * 3, *pieces, labels)
    own = own + send(own, plan.pairs(plan.core))
    own = own + send(own, plan.pairs(plan.side))
    sums = own[rows:]

    inner, outer = [], []
    for k in range(2):
        inner.append(send(near[k], plan.pairs(plan.inner)))
        passed = call(functools.partial(pick_kernel, plan.mask(plan.far_end)), piece, [whole] * 2, pieces[k], near[k])
        outer.append(send(passed, plan.pairs(plan.outer)))

    mine = call(near_kernel, tile, [whole] * 5, *pieces, labels, *near)
    passed = send(mine, plan.pairs(plan.cross))
    theirs = send(mine, plan.pairs(plan.core))
    early = call(
        functools.partial(early_kernel, roles["mine"], roles["beside"]), tile, [whole] * 3, mine, theirs, passed
    )
    swapped = send(sums, plan.pairs(plan.swap))

    far_specs = [[whole, half_labels[k], whole, whole] for k in range(2)]
    far = call(
        functools.partial(far_first_kernel, roles["hub"]), two_tiles, far_specs[0],
        pieces[0], labels, inner[0], outer[0],
    )
    late = plan.late_pairs()
    *outs, keep = call(
        functools.partial(far_second_kernel, roles), [tile] * (len(late) + 1), far_specs[1] + [whole],
        pieces[1], labels, inner[1], outer[1], far,
    )
    outs[0] = call(functools.partial(pick_kernel, roles["early"]), tile, [whole] * 2, early, outs[0])
    got = [send(out, pairs) for pairs, out in zip(late, outs)]
    return call(
        functools.partial(final_kernel, pix_total, roles),
        jax.ShapeDtypeStruct((CYCLES, frames, frames), jnp.float32), [whole] * 9,
        keep, early, own, *got, sums, swapped,
    )


def ring_body(intensity, cycle_labels):
    frames_dev, pix_dev = intensity.shape
    pix_total = pix_dev * lax.axis_size("pix")
    cycles = jnp.arange(CYCLES, dtype=cycle_labels.dtype)
    keep = cycle_labels[None, :] == cycles[:, None]
    grouped = jnp.where(keep[:, None, :], intensity[None], 0)
    local_sums = jnp.sum(grouped, axis=2, dtype=jnp.float32)
    cycle_sum = lax.psum(local_sums, "pix")
    frame_sums = lax.all_gather(cycle_sum, "tm", axis=1, tiled=True)
    blocks_count = lax.axis_size("tm")
    frames = frames_dev * blocks_count
    myself = lax.axis_index("tm")
    pairs = [(source, (source + 1) % blocks_count) for source in range(blocks_count)]

    def place(row, block, source):
        tile = jnp.einsum("qap,bp->qab", grouped, block, preferred_element_type=jnp.float32)
        return lax.dynamic_update_slice(row, tile, (0, 0, source * frames_dev))

    def turn(step, carry):
        block, row_now = carry
        row_now = place(row_now, block, (myself - step) % blocks_count)
        return (lax.ppermute(block, "tm", pairs), row_now)

    row = jnp.zeros((CYCLES, frames_dev, frames), jnp.float32)
    block, row = lax.fori_loop(0, blocks_count - 1, turn, (intensity, row))
    row = place(row, block, (myself + 1) % blocks_count)
    columns = frames // lax.axis_size("pix")
    start = lax.axis_index("pix") * columns
    gram = lax.psum_scatter(row, "pix", scatter_dimension=2, tiled=True)
    column_sums = lax.dynamic_slice_in_dim(frame_sums, start, columns, 1)
    return (pix_total // CYCLES) * gram / (cycle_sum[:, :, None] * column_sums[:, None, :])


def solution(mesh):
    placed = (P(("win", "tm"), "pix"), P("pix"))
    planned = mesh.shape["tm"] == 4 and mesh.shape["pix"] == 4 and mesh.shape["win"] % 2 == 0

    def body(intensity, cycle_labels):
        return (planned_body if planned else ring_body)(intensity, cycle_labels)

    return jax.shard_map(body, mesh=mesh, in_specs=placed, out_specs=P("win", "tm", "pix"), check_vma=False)
```

```python
import functools

import jax
import jax.numpy as jnp
from jax import lax
from jax.experimental import pallas as pl
from jax.experimental.pallas import tpu as pltpu
from jax.sharding import PartitionSpec as P


CYCLES = 2
SUM_ROWS = 16
TILE, ENDS, EARLY = 0, 1, 2
LINE = ("win", "tm", "pix")
SLOTS = (2, 0, 1, 3, 3, 2, 0, 0, 2, 3, 1, 0)
CONTRACT_LAST = (((1,), (1,)), ((), ()))


def masks_of(labels, rows):
    cycle = lax.broadcasted_iota(jnp.int32, (rows, labels.shape[-1]), 0)
    return (cycle == labels).astype(jnp.float32).astype(jnp.bfloat16)


def masked(block, masks):
    return [block * masks[q : q + 1, :] for q in range(CYCLES)]


def products(left, right):
    return lax.dot_general(left, right, CONTRACT_LAST, preferred_element_type=jnp.float32)


def chosen(mask, value_if, value_else):
    return jnp.where(bit(mask) == 1, value_if, value_else)


def bit(mask):
    place = lax.axis_index("tm") * lax.axis_size("pix") + lax.axis_index("pix")
    return (jnp.int32(mask) >> place) & 1


def cut_kernel(k, x_ref, out_ref, sem):
    half = out_ref.shape[1]
    copy = pltpu.make_async_copy(x_ref.at[:, k * half : (k + 1) * half], out_ref, sem)
    copy.start()
    copy.wait()


def pick_kernel(mask, if_ref, else_ref, out_ref):
    out_ref[...] = chosen(mask, if_ref[...], else_ref[...])


def early_kernel(near_side, beside, mine_ref, theirs_ref, passed_ref, out_ref):
    total = chosen(near_side, mine_ref[...], theirs_ref[...]) + passed_ref[...]
    out_ref[...] = chosen(beside, total, 0.0)


def own_kernel(first_ref, second_ref, labels_ref, out_ref):
    masks = masks_of(labels_ref[...], SUM_ROWS)
    half = first_ref.shape[1]
    total = None
    for k, ref in enumerate((first_ref, second_ref)):
        x, here = ref[...], masks[:, k * half : (k + 1) * half]
        part = products(jnp.concatenate(masked(x, here) + [here], axis=0), x)
        total = part if total is None else total + part
    out_ref[...] = total


def near_kernel(first_ref, second_ref, labels_ref, near_first_ref, near_second_ref, out_ref):
    masks = masks_of(labels_ref[...], SUM_ROWS)
    half = first_ref.shape[1]
    total = None
    for k, (ref, near_ref) in enumerate(((first_ref, near_first_ref), (second_ref, near_second_ref))):
        part = products(jnp.concatenate(masked(ref[...], masks[:, k * half : (k + 1) * half]), axis=0), near_ref[...])
        total = part if total is None else total + part
    out_ref[...] = total


def far_products(hub, x_ref, labels_ref, inner_ref, outer_ref):
    masks = masks_of(labels_ref[...], SUM_ROWS)
    outer = outer_ref[...]
    met = chosen(hub, inner_ref[...], outer)
    return products(jnp.concatenate([x_ref[...], outer], axis=0), jnp.concatenate(masked(met, masks), axis=0))


def far_first_kernel(hub, x_ref, labels_ref, inner_ref, outer_ref, out_ref):
    out_ref[...] = far_products(hub, x_ref, labels_ref, inner_ref, outer_ref)


def far_second_kernel(roles, x_ref, labels_ref, inner_ref, outer_ref, sofar_ref, *rest):
    outs, keep_ref = rest[:-1], rest[-1]
    frames = x_ref.shape[0]
    far = sofar_ref[...] + far_products(roles["hub"], x_ref, labels_ref, inner_ref, outer_ref)
    for q in range(CYCLES):
        part = slice(q * frames, (q + 1) * frames)
        tile, ends = far[:frames, part], far[frames:, part]
        keep_ref[part, :] = chosen(roles["keep"], tile, 0.0)
        for slot, out_ref in enumerate(outs):
            out_ref[part, :] = chosen(roles["ends"][slot], ends, tile)


def final_kernel(pix_total, roles, keep_ref, early_ref, own_ref, sums_ref, swapped_ref, *rest):
    got, out_ref = rest[:-1], rest[-1]
    frames = out_ref.shape[1]
    sums = sums_ref[...]
    columns = chosen(roles["diagonal"], sums, swapped_ref[...])
    for q in range(CYCLES):
        part = slice(q * frames, (q + 1) * frames)
        gram = keep_ref[part, :] + early_ref[part, :] + chosen(roles["diagonal"], own_ref[part, :], 0.0)
        turned = jnp.zeros_like(gram)
        for ref, turned_here, straight_here in zip(got, roles["turned"], roles["straight"]):
            tile = ref[part, :]
            if turned_here:
                turned = turned + chosen(turned_here, tile, 0.0)
            if straight_here:
                gram = gram + chosen(straight_here, tile, 0.0)
        gram = gram + turned.T
        row_sum = jnp.broadcast_to(sums[q : q + 1, :], (frames, frames)).T
        out_ref[q] = (pix_total // CYCLES) * gram / (row_sum * columns[q : q + 1, :])


def vmem_call(kernel, out_shapes, in_specs, flops, bytes_accessed, scratch=(), limit=16 * 2**20):
    many = isinstance(out_shapes, (list, tuple))
    whole = pl.BlockSpec(memory_space=pltpu.VMEM)
    return pl.pallas_call(
        kernel,
        out_shape=out_shapes,
        grid=(1,),
        in_specs=in_specs,
        out_specs=[whole] * len(out_shapes) if many else whole,
        scratch_shapes=scratch,
        compiler_params=pltpu.CompilerParams(vmem_limit_bytes=limit),
        cost_estimate=pl.CostEstimate(flops=flops, bytes_accessed=bytes_accessed, transcendentals=0),
    )


def completed(count, edges, cost):
    target_of = dict(edges)
    free = [s for s in range(count) if s not in target_of]
    open_targets = [t for t in range(count) if t not in set(target_of.values())]
    size = len(free)
    price = [[cost(s, t) for t in open_targets] for s in free]
    row_cost, column_cost = [0] * (size + 1), [0] * (size + 1)
    owner, back = [0] * (size + 1), [0] * (size + 1)
    for row in range(1, size + 1):
        owner[0], column = row, 0
        least, done = [float("inf")] * (size + 1), [False] * (size + 1)
        while owner[column]:
            done[column] = True
            here, step, following = owner[column], float("inf"), 0
            for j in range(1, size + 1):
                if not done[j]:
                    value = price[here - 1][j - 1] - row_cost[here] - column_cost[j]
                    if value < least[j]:
                        least[j], back[j] = value, column
                    if least[j] < step:
                        step, following = least[j], j
            for j in range(size + 1):
                if done[j]:
                    row_cost[owner[j]] += step
                    column_cost[j] -= step
                else:
                    least[j] -= step
            column = following
        while column:
            owner[column] = owner[back[column]]
            column = back[column]
    for j in range(1, size + 1):
        target_of[free[owner[j] - 1]] = open_targets[j - 1]
    return sorted(target_of.items())


class Plan:
    def __init__(self, windows, blocks):
        self.windows = windows
        self.last = blocks - 1
        self.places = [(z, x, c) for z in range(blocks) for x in range(2) for c in range(2)]
        self.devices = [(w,) + place for w in range(windows) for place in self.places]

    def index(self, device):
        return self.devices.index(device)

    def pairs(self, rule):
        found = []
        for device in self.devices:
            place = rule(*device[1:])
            target = (device[0] ^ 1,) + device[1:] if place is None else (device[0],) + place
            found.append((self.index(device), self.index(target)))
        return found

    def mask(self, rule):
        return sum(1 << k for k, place in enumerate(self.places) if rule(*place))

    def shift(self, z, x, c):
        t = z + 1 - 2 * c
        return (t, x, c) if 0 <= t <= self.last else (z, x, 1 - c)

    def hub(self, z, x, c):
        return z == 2 - c

    def far_end(self, z, x, c):
        return z == (self.last if c == 0 else 0)

    def inner(self, z, x, c):
        return (2 - c, x, c) if z == 1 + c else (z, x, 1 - c)

    def outer(self, z, x, c):
        if self.hub(z, x, c):
            return (z + 1 - 2 * c, x, c)
        if self.far_end(z, x, c):
            return (z - 1 + 2 * c, x, c)
        return None

    def core(self, z, x, c):
        return (z, x, 1 - c)

    def side(self, z, x, c):
        return (z, 1 - x, c)

    def cross(self, z, x, c):
        return (z, 1 - x, 1 - c if x == z // 2 else c)

    def swap(self, z, x, c):
        return None if 2 * x + c == z else (2 * x + c, z // 2, z % 2)

    def late(self):
        a, b, c, d = (2, 0, 0), (2, 1, 0), (0, 0, 1), (0, 1, 1)
        lower, upper = (0, 1, 0), (2, 0, 0)
        corner, other = (0, 1, 1), (3, 0, 0)
        edges = [
            (a, lower, TILE, True), (b, lower, TILE, True), (c, lower, TILE, False), (d, lower, TILE, False),
            (b, upper, TILE, False), (c, upper, TILE, True), (d, upper, TILE, True),
            (a, corner, ENDS, True), (b, corner, ENDS, True), (a, other, ENDS, False), (b, other, ENDS, False),
        ]

        def mirror(place):
            z, x, k = place
            return (self.last - z, 1 - x, 1 - k)

        slots = [{} for _ in range(4)]
        for slot, (source, target, tile, turned) in zip(SLOTS, edges):
            slots[slot][source] = (target, tile, turned)
            slots[slot][mirror(source)] = (mirror(target), tile, turned)
        for place in self.places:
            z, x, c = place
            if abs(2 * x + c - z) == 1:
                slots[SLOTS[-1]][place] = (self.swap(*place), EARLY, True)
        return slots

    def links(self, source, target):
        (w, z, x, c), (tw, tz, tx, tc) = source, target
        step = 1 if tz > z else -1
        found = [("block", w, x, here, step) for here in range(z, tz, step)]
        if tx != x:
            found.append(("side", w, tz, x))
        if tw != w:
            found.append(("window", w, tz, tx))
        return found

    def late_pairs(self):
        load, slots = {}, []

        def carry(source, target):
            for link in self.links(source, target):
                load[link] = load.get(link, 0) + 1

        for slot in self.late():
            edges = [
                ((w,) + source, (w,) + target) for w in range(self.windows) for source, (target, _, _) in slot.items()
            ]
            for edge in edges:
                carry(*edge)
            slots.append([(self.index(source), self.index(target)) for source, target in edges])

        def cost(source, target):
            if source == target:
                return 10**6
            places = self.devices[source], self.devices[target]
            return 1 + sum(
                (20 if link[0] == "block" else 10) + 10 * load.get(link, 0) ** 2 for link in self.links(*places)
            )

        result = []
        for edges in slots:
            pairs = completed(len(self.devices), edges, cost)
            for source, target in set(pairs) - set(edges):
                carry(self.devices[source], self.devices[target])
            result.append(pairs)
        return result

    def roles(self):
        late = self.late()

        def picks(slot, value):
            return self.mask(lambda *place: place in slot and slot[place][1] == value)

        def arrivals(slot, turned):
            targets = [target for target, _, kind in slot.values() if kind == turned]
            return self.mask(lambda *place: place in targets)

        return {
            "hub": self.mask(self.hub),
            "keep": self.mask(lambda *place: place in ((2, 0, 0), (1, 1, 1))),
            "diagonal": self.mask(lambda z, x, c: 2 * x + c == z),
            "beside": self.mask(lambda z, x, c: abs(2 * x + c - z) == 1),
            "mine": self.mask(lambda z, x, c: x == z // 2),
            "ends": [picks(slot, ENDS) for slot in late],
            "early": picks(late[SLOTS[-1]], EARLY),
            "turned": [arrivals(slot, True) for slot in late],
            "straight": [arrivals(slot, False) for slot in late],
        }


def planned_body(intensity, cycle_labels):
    frames, pix_dev = intensity.shape
    half = pix_dev // 2
    pix_total = pix_dev * lax.axis_size("pix")
    plan = Plan(lax.axis_size("win"), lax.axis_size("tm"))
    roles = plan.roles()

    def send(value, pairs):
        return lax.ppermute(value, LINE, pairs)

    def call(kernel, shapes, specs, *args, **options):
        return vmem_call(kernel, shapes, specs, work, block_bytes, **options)(*args)

    labels = cycle_labels.reshape(1, pix_dev)
    whole = pl.BlockSpec(memory_space=pltpu.VMEM)
    half_labels = [pl.BlockSpec((1, half), lambda step, k=k: (0, k)) for k in range(2)]
    rows = CYCLES * frames
    tile = jax.ShapeDtypeStruct((rows, frames), jnp.float32)
    tile_sums = jax.ShapeDtypeStruct((rows + SUM_ROWS, frames), jnp.float32)
    two_tiles = jax.ShapeDtypeStruct((2 * frames, rows), jnp.float32)
    piece = jax.ShapeDtypeStruct((frames, half), intensity.dtype)
    work = 2 * rows * frames * pix_dev
    block_bytes = 2 * frames * pix_dev

    held = pltpu.with_memory_space_constraint(intensity, pltpu.HBM)
    pieces, near = [], []
    for k in range(2):
        cut = functools.partial(cut_kernel, k)
        in_hbm = pl.BlockSpec(memory_space=pltpu.HBM)
        pieces.append(call(cut, piece, [in_hbm], held, scratch=[pltpu.SemaphoreType.DMA]))
        near.append(send(pieces[k], plan.pairs(plan.shift)))

    own = call(own_kernel, tile_sums, [whole] * 3, *pieces, labels)
    own = own + send(own, plan.pairs(plan.core))
    own = own + send(own, plan.pairs(plan.side))
    sums = own[rows:]

    inner, outer = [], []
    for k in range(2):
        inner.append(send(near[k], plan.pairs(plan.inner)))
        passed = call(functools.partial(pick_kernel, plan.mask(plan.far_end)), piece, [whole] * 2, pieces[k], near[k])
        outer.append(send(passed, plan.pairs(plan.outer)))

    mine = call(near_kernel, tile, [whole] * 5, *pieces, labels, *near)
    passed = send(mine, plan.pairs(plan.cross))
    theirs = send(mine, plan.pairs(plan.core))
    early = call(
        functools.partial(early_kernel, roles["mine"], roles["beside"]), tile, [whole] * 3, mine, theirs, passed
    )
    swapped = send(sums, plan.pairs(plan.swap))

    far_specs = [[whole, half_labels[k], whole, whole] for k in range(2)]
    far = call(
        functools.partial(far_first_kernel, roles["hub"]), two_tiles, far_specs[0],
        pieces[0], labels, inner[0], outer[0],
    )
    late = plan.late_pairs()
    *outs, keep = call(
        functools.partial(far_second_kernel, roles), [tile] * (len(late) + 1), far_specs[1] + [whole],
        pieces[1], labels, inner[1], outer[1], far,
    )
    ride = SLOTS[-1]
    outs[ride] = call(functools.partial(pick_kernel, roles["early"]), tile, [whole] * 2, early, outs[ride])
    got = [send(out, pairs) for pairs, out in zip(late, outs)]
    return call(
        functools.partial(final_kernel, pix_total, roles),
        jax.ShapeDtypeStruct((CYCLES, frames, frames), jnp.float32), [whole] * 9,
        keep, early, own, sums, swapped, *got,
    )


def ring_body(intensity, cycle_labels):
    frames_dev, pix_dev = intensity.shape
    pix_total = pix_dev * lax.axis_size("pix")
    cycles = jnp.arange(CYCLES, dtype=cycle_labels.dtype)
    keep = cycle_labels[None, :] == cycles[:, None]
    grouped = jnp.where(keep[:, None, :], intensity[None], 0)
    local_sums = jnp.sum(grouped, axis=2, dtype=jnp.float32)
    cycle_sum = lax.psum(local_sums, "pix")
    frame_sums = lax.all_gather(cycle_sum, "tm", axis=1, tiled=True)
    blocks_count = lax.axis_size("tm")
    frames = frames_dev * blocks_count
    myself = lax.axis_index("tm")
    pairs = [(source, (source + 1) % blocks_count) for source in range(blocks_count)]

    def place(row, block, source):
        tile = jnp.einsum("qap,bp->qab", grouped, block, preferred_element_type=jnp.float32)
        return lax.dynamic_update_slice(row, tile, (0, 0, source * frames_dev))

    def turn(step, carry):
        block, row_now = carry
        row_now = place(row_now, block, (myself - step) % blocks_count)
        return (lax.ppermute(block, "tm", pairs), row_now)

    row = jnp.zeros((CYCLES, frames_dev, frames), jnp.float32)
    block, row = lax.fori_loop(0, blocks_count - 1, turn, (intensity, row))
    row = place(row, block, (myself + 1) % blocks_count)
    columns = frames // lax.axis_size("pix")
    start = lax.axis_index("pix") * columns
    gram = lax.psum_scatter(row, "pix", scatter_dimension=2, tiled=True)
    column_sums = lax.dynamic_slice_in_dim(frame_sums, start, columns, 1)
    return (pix_total // CYCLES) * gram / (cycle_sum[:, :, None] * column_sums[:, None, :])


def solution(mesh):
    placed = (P(("win", "tm"), "pix"), P("pix"))
    planned = mesh.shape["tm"] == 4 and mesh.shape["pix"] == 4 and mesh.shape["win"] % 2 == 0

    def body(intensity, cycle_labels):
        return (planned_body if planned else ring_body)(intensity, cycle_labels)

    return jax.shard_map(body, mesh=mesh, in_specs=placed, out_specs=P("win", "tm", "pix"), check_vma=False)
```
